32 devices in a mesh: row: 4 (over y, x), col: 8 (over z, core).
Axes of the slice: x: 2, y: 2, z: 4, core: 2. Of those that a mesh axis runs over, the one named last changes fastest.
Arguments:
- inverses: bfloat16 [4, 32, 1024, 1024], P('row', 'col'), as said below
- coupling: bfloat16 [4, 32, 1024, 256], P('row', 'col'), may hold values from -0.1875 to 0.1875
- orders: int32 [4, 32], P('row', 'col'), may hold values from 512 to 1024, as said below
- owners: int32 [4, 32, 1], P(None, 'col'), may hold values from 0 to 3, as said below
- offsets: int32 [4, 32, 2], P(None, 'col'), may hold values from 0 to 2
- dense_slab: float32 [2048, 4096], P('row', 'col'), may hold values from -6 to 6
- pivots: float32 [1024], replicated, may hold values from 16 to 128
Outputs:
- result: float32 [2048, 4096], P('row', 'col')
The draws below stay inside these ranges and needn't reach their ends.
Inputs may be any that keep to these rules, and one draw needn't show every extreme that they name: `orders`: order of each subdomain; some subdomain has exactly 1024. `owners`: within the 4 subdomains of one device (entries r, s with the same r and the same s // 4) no row block is named twice. `inverses`: each inverse is symmetric.
All inputs are finite; a program needn't handle non-finite values.
Results may differ from the reference program's by a relative error of at most 0.0035.
Values may be sent and summed in bfloat16 or wider, within the bound.
A program may use at most 64 MiB of HBM per device.

```python
import math
import jax
import jax.numpy as jnp
from jax import lax

ORD = 1024
KC = 256
TILE = 512
PW = 1024
SUBS = 4
NSUB_ROW = 32
OFF_UNIT = 128
ROWS = 2048
COLS = 4096
N_ROW = 4


def draw_inverses(key, part):
    shape = (N_ROW, NSUB_ROW, ORD, ORD)
    noise = jax.random.normal(key, shape, jnp.float32)
    symmetric = (noise + jnp.swapaxes(noise, 2, 3)) * (0.6 / ORD ** 0.5)
    identity = jnp.eye(ORD, dtype=jnp.float32)
    return (symmetric + identity).astype(jnp.bfloat16)


def draw_orders(key, part):
    values = jax.random.randint(key, (N_ROW, NSUB_ROW), ORD // 2, ORD + 1, jnp.int32)
    return values.at[0, 0].set(ORD)


def draw_owners(key, part):
    device_count = N_ROW * (NSUB_ROW // SUBS)
    device_keys = jax.random.split(jax.random.fold_in(key, 7), device_count)

    def pick(one_key):
        return jax.random.permutation(one_key, N_ROW)[:SUBS].astype(jnp.int32)
    chosen = jax.vmap(pick)(device_keys)
    return chosen.reshape(N_ROW, NSUB_ROW, 1)


def set_ends(array, rng, smallest, high):
    place = [jax.random.randint(jax.random.fold_in(rng, axis), (), 0, length) for axis, length in enumerate(array.shape)]
    widest = array.shape.index(max(array.shape))
    neighbour = place[:widest] + [(place[widest] + 1) % array.shape[widest]] + place[widest + 1:]
    return array.at[tuple(place)].set(smallest).at[tuple(neighbour)].set(high)


def levels(rng, dims, cuts, least, top_value):
    def one(dim, blocks):
        steps = jax.random.uniform(jax.random.fold_in(jax.random.fold_in(rng, 6), dim), (blocks,), jnp.float32, least / len(cuts), top_value / len(cuts))
        return jnp.repeat(jnp.exp(steps), dims[dim] // blocks).reshape((-1,) + (1,) * (len(dims) - dim - 1))

    loudness = one(*cuts[0])
    for cut in cuts[1:]:
        loudness = loudness * one(*cut)
    return loudness


def bell_draw(stream_key, shape, width, limit, shards=(), kind=jnp.bfloat16):
    entries = width * jax.random.normal(stream_key, shape, jnp.float32)
    if shards:
        entries = entries * levels(stream_key, shape, shards, -0.22, 0.18)
    return jnp.clip(entries, -limit, limit).astype(kind)


def setup_inputs(seed: int = 0) -> dict:
    seeds = jax.random.split(jax.random.key(seed), 8)
    return {
        "inverses": draw_inverses(jax.random.fold_in(seeds[7], 71), 0),
        "coupling": bell_draw(seeds[1], (N_ROW, NSUB_ROW, ORD, KC), ORD ** -0.5, 0.1875, ((0, 4), (1, 8))),
        "orders": draw_orders(jax.random.fold_in(seeds[7], 71), 0),
        "owners": draw_owners(jax.random.fold_in(seeds[7], 71), 0),
        "offsets": set_ends(jax.random.randint(seeds[4], (N_ROW, NSUB_ROW, 2), 0, 3), jax.random.fold_in(seeds[4], 1), 0, 2).astype(jnp.int32),
        "dense_slab": bell_draw(seeds[5], (ROWS, COLS), 1.0, 6.0, ((0, 4), (1, 8)), jnp.float32),
        "pivots": jnp.clip(jnp.exp(jax.random.uniform(seeds[6], (PW,), jnp.float32, math.log(16.0), math.log(128.0))), 16.0, 128.0),
    }


def make_tile(inverse, coupling_cols, order_size):
    live_rows = jnp.arange(inverse.shape[0], dtype=jnp.int32)[:, None] < order_size
    masked = jnp.where(live_rows, coupling_cols, jnp.zeros_like(coupling_cols))
    solved = jnp.dot(inverse.astype(jnp.float32), masked.astype(jnp.float32)).astype(jnp.bfloat16)
    return jnp.dot(masked.astype(jnp.float32).T, solved.astype(jnp.float32)).astype(jnp.bfloat16)


def reference(inverses, coupling, orders, owners, offsets, dense_slab, pivots):
    def add_one(counter, schur_sum):
        row_index = counter // NSUB_ROW
        sub_index = counter % NSUB_ROW
        tile_value = make_tile(inverses[row_index, sub_index], coupling[row_index, sub_index], orders[row_index, sub_index])
        row_start = (owners[row_index, sub_index, 0] * TILE + offsets[row_index, sub_index, 0] * OFF_UNIT).astype(jnp.int32)
        col_start = ((sub_index // SUBS) * TILE + offsets[row_index, sub_index, 1] * OFF_UNIT).astype(jnp.int32)
        current = lax.dynamic_slice(schur_sum, (row_start, col_start), (KC, KC))
        return lax.dynamic_update_slice(schur_sum, current + tile_value.astype(schur_sum.dtype), (row_start, col_start))

    schur_sum = lax.fori_loop(0, N_ROW * NSUB_ROW, add_one, jnp.zeros(dense_slab.shape, jnp.float32))
    updated = dense_slab - schur_sum
    panel = updated[:PW].astype(jnp.bfloat16)
    left_factor = (panel[:, :N_ROW * TILE].astype(jnp.float32) / pivots[:, None]).astype(jnp.bfloat16)
    return updated - jnp.dot(left_factor.astype(jnp.float32).T, panel.astype(jnp.float32))
```

```python
import functools
import jax
import jax.numpy as jnp
from jax import lax
from jax.experimental import pallas as pl
from jax.experimental.pallas import tpu as pltpu
from jax.sharding import PartitionSpec as P

MESH = pl.DeviceIdType.MESH
BF16 = jnp.bfloat16
F32 = jnp.float32
CHUNKS = 16
MERGE = 2
AB = 256
PAD = 16
HOP_ROW = 8
HOP_COL = 8
HOP_CORE = 5


def contract0(a, b):
    return lax.dot_general(a, b, (((0,), (0,)), ((), ())), preferred_element_type=F32)


def kernel(
    dims,
    inv_hbm, cpl_hbm, orders, owners, offsets, slab_hbm, pivots,
    out,
    a_buf, m_buf, slab, send, recv, placed, panel, left, piv,
    a_sem, m_sem, s_sem, t_send, t_recv, ax_send, ay_send, g_recv,
    up_send, dn_send, core_send, l_recv,
):
    rows, cols, subs, order, width, tile = dims
    unit = (tile - width) // 2
    nb = width // unit
    grid = tile // unit
    pairs = [(a, b) for a in range(nb) for b in range(a + 1, nb)]
    chunk = tile // CHUNKS
    ablocks = order // AB

    r = lax.axis_index("row")
    c = lax.axis_index("col")
    q, core = lax.div(c, 2), lax.rem(c, 2)
    chips = cols // 2
    q0, k0 = lax.div(r, 2), lax.rem(r, 2)
    pa = lax.rem(r, 2)
    pb = 1 - pa
    mate = r + 1 - 2 * pa
    sibling = c + 1 - 2 * core
    on_line = core == k0
    at_source = q == q0
    diag = at_source & on_line
    has_up = (q >= q0) & (q + 1 < chips)
    has_dn = (q <= q0) & (q > 0)
    chip_hops = jnp.where(q >= q0, q - q0, q0 - q)
    pc = jnp.where(on_line, pb, pa)
    po = 1 - pc

    def load_a(s, i):
        return pltpu.make_async_copy(
            inv_hbm.at[0, s, pl.ds(i * AB, AB), pl.ds(i * AB, order - i * AB)],
            a_buf.at[s, pl.ds(i * AB, AB), pl.ds(i * AB, order - i * AB)],
            a_sem.at[s])

    def wait_a(s):
        total = sum(AB * (order - i * AB) for i in range(ablocks)) // order
        pltpu.make_async_copy(
            inv_hbm.at[0, s, pl.ds(0, total)], a_buf.at[s, pl.ds(0, total)], a_sem.at[s]).wait()

    def load_m(s):
        return pltpu.make_async_copy(cpl_hbm.at[0, s], m_buf.at[s], m_sem.at[s])

    load_slab = pltpu.make_async_copy(slab_hbm, slab, s_sem)
    for s in range(subs):
        load_m(s).start()
        for i in range(ablocks):
            load_a(s, i).start()

    barrier = pltpu.get_barrier_semaphore()
    for t in range(rows):
        @pl.when(t != r)
        def _():
            pl.semaphore_signal(barrier, inc=1, device_id=(t, c), device_id_type=MESH)
    pl.semaphore_signal(barrier, inc=1, device_id=(r, sibling), device_id_type=MESH)

    @pl.when(q + 1 < chips)
    def _():
        pl.semaphore_signal(barrier, inc=1, device_id=(r, c + 2), device_id_type=MESH)

    @pl.when(q > 0)
    def _():
        pl.semaphore_signal(barrier, inc=1, device_id=(r, c - 2), device_id_type=MESH)

    def pick(src, dst):
        found, which = jnp.int32(0), jnp.int32(0)
        for s in range(subs):
            hit = owners[src, 0, s] == dst
            found, which = jnp.where(hit, 1, found), jnp.where(hit, s, which)
        return found, which

    def tile_copy(t, src_row):
        return pltpu.make_async_remote_copy(
            src_ref=send.at[t], dst_ref=recv.at[src_row],
            send_sem=t_send, recv_sem=t_recv.at[src_row],
            device_id=(t, c), device_id_type=MESH)

    above = (lax.broadcasted_iota(jnp.int32, (unit, unit), 0)
             <= lax.broadcasted_iota(jnp.int32, (unit, unit), 1))
    equal = (lax.broadcasted_iota(jnp.int32, (unit, unit), 0)
             == lax.broadcasted_iota(jnp.int32, (unit, unit), 1))

    def make_tile(which):
        live = lax.broadcasted_iota(jnp.int32, (order, width), 0) < orders[0, which]
        masked = jnp.where(live, m_buf[which], jnp.zeros((order, width), BF16))
        pieces = []
        for i in range(ablocks):
            lo, hi = i * AB, (i + 1) * AB
            half = a_buf[which, lo:hi, lo:hi] * jnp.asarray(0.5, BF16)
            piece = jnp.dot(half, masked[lo:hi], preferred_element_type=F32)
            if hi < order:
                piece = piece + jnp.dot(a_buf[which, lo:hi, hi:], masked[hi:],
                                        preferred_element_type=F32)
            pieces.append(piece.astype(BF16))
        half_tile = contract0(masked, jnp.concatenate(pieces, axis=0))

        def block(a, b):
            return half_tile[a * unit:(a + 1) * unit, b * unit:(b + 1) * unit]

        def whole(a, b):
            return block(a, b) + jnp.transpose(block(b, a))

        stored = [jnp.where(above, whole(a, a), whole(a + 1, a + 1)) for a in range(0, nb, 2)]
        stored += [whole(a, b) for a, b in pairs]
        stored += [jnp.broadcast_to(jnp.sum(jnp.where(equal, 2 * block(a, a), 0.0), axis=0, keepdims=True),
                                    (PAD, unit)) for a in range(1, nb, 2)]
        return jnp.concatenate(stored, axis=0).astype(BF16)

    for s in range(subs):
        load_m(s).wait()
        wait_a(s)
    load_slab.start()

    neighbours = rows + jnp.where(q + 1 < chips, 1, 0) + jnp.where(q > 0, 1, 0)
    pl.semaphore_wait(barrier, neighbours)

    others = rows - 2
    for u in range(rows):
        if u == 0:
            t = pb
        elif u == rows - 1:
            t = r
        else:
            far = jnp.where(r < 2, 2 + lax.rem(u - 1 + pa, others), 2 + lax.rem(r - 2 + u - 1, others))
            t = jnp.where(r >= 2, pa, far) if u == 1 else far
        _, which = pick(r, t)
        value = make_tile(which)
        if u < rows - 1:
            send[t] = value
            tile_copy(t, r).start()
        else:
            recv[t] = value

    for k in range(pivots.shape[0]):
        piv[pl.ds(k * 128, 128), :] = jnp.transpose(
            jnp.broadcast_to(pivots[pl.ds(k, 1), :], (128, 128)))
    for t in range(rows):
        for k in range(nb + 1):
            placed[t, k * (nb + 1) + nb] = jnp.zeros((unit, unit), BF16)
            placed[t, nb * (nb + 1) + k] = jnp.zeros((unit, unit), BF16)


    def part(ref, p, j):
        return ref.at[p, pl.ds(pl.multiple_of(j * chunk, chunk), chunk)]

    def panel_copy(j, target, sem):
        return pltpu.make_async_remote_copy(
            src_ref=part(panel, pa, j), dst_ref=part(panel, pa, j),
            send_sem=sem, recv_sem=g_recv.at[pa, j],
            device_id=(target, c), device_id_type=MESH)

    def panel_got(p, j):
        pltpu.make_async_remote_copy(
            src_ref=part(panel, p, j), dst_ref=part(panel, p, j),
            send_sem=ax_send, recv_sem=g_recv.at[p, j],
            device_id=(mate, c), device_id_type=MESH).wait_recv()

    def send_panel(j):
        panel_copy(j, mate, ax_send).start()

        @pl.when(r + 2 < rows)
        def _():
            panel_copy(j, r + 2, ay_send).start()

    def left_copy(p, j, target, sem):
        return pltpu.make_async_remote_copy(
            src_ref=part(left, p, j), dst_ref=part(left, p, j),
            send_sem=sem, recv_sem=l_recv.at[p, j],
            device_id=(r, target), device_id_type=MESH)

    def along(j):
        @pl.when(has_up)
        def _():
            left_copy(pc, j, c + 2, up_send).start()

        @pl.when(has_dn)
        def _():
            left_copy(pc, j, c - 2, dn_send).start()

    lanes = tile // 128

    def divide(p, j):
        at = pl.ds(pl.multiple_of(j * chunk, chunk), chunk)
        pivot = piv[pl.ds(pl.multiple_of(p * tile + j * chunk, chunk), chunk), :]
        raw = panel[p, at].astype(F32)
        left[p, at] = (raw / jnp.concatenate([pivot] * lanes, axis=1)).astype(BF16)

    load_slab.wait()
    places = []
    side = nb + 1
    for t in range(rows):
        found, which = pick(t, r)
        at_row, at_col = offsets[t, 0, which], offsets[t, 1, which]
        spots = []
        for start in (at_row, at_col):
            inside = [(found > 0) & (k - start >= 0) & (k - start < nb) for k in range(grid)]
            spots.append([jnp.where(ok, k - start, nb) for k, ok in enumerate(inside)])
        places.append(([side * a for a in spots[0]], spots[1]))

        @pl.when(t != r)
        def _():
            tile_copy(t, t).wait_recv()
    for t in range(rows):
        for k in range(nb // 2):
            pack = recv[t, k * unit:(k + 1) * unit].astype(F32)
            flip = jnp.transpose(pack)
            at = (nb // 2 + len(pairs)) * unit + k * PAD
            line = jnp.concatenate([recv[t, at:at + PAD]] * (unit // PAD), axis=0).astype(F32)
            a = 2 * k
            placed[t, a * side + a] = jnp.where(above, pack, flip).astype(BF16)
            low = jnp.where(above, flip, pack)
            placed[t, (a + 1) * side + a + 1] = jnp.where(equal, line, low).astype(BF16)
        for k, (a, b) in enumerate(pairs):
            at = (nb // 2 + k) * unit
            value = recv[t, at:at + unit]
            placed[t, a * side + b] = value
            placed[t, b * side + a] = jnp.transpose(value.astype(F32)).astype(BF16)
    for i in range(grid):
        for j in range(grid):
            total = slab[i * unit:(i + 1) * unit, j * unit:(j + 1) * unit]
            for t in range(rows):
                total = total - placed[t, places[t][0][i] + places[t][1][j]].astype(F32)
            out[i * unit:(i + 1) * unit, j * unit:(j + 1) * unit] = total

        @pl.when(r < 2)
        def _():
            span = slice(i * unit, (i + 1) * unit)
            panel[pa, span] = out[span, :].astype(BF16)
            for j in range(i * unit // chunk, (i + 1) * unit // chunk):
                send_panel(j)

    row_hops = lax.div(r, 2)
    at_pa = HOP_ROW * row_hops
    at_pb = at_pa + HOP_ROW
    line_pa = at_pa + HOP_CORE + HOP_COL * chip_hops
    line_pb = at_pb + HOP_COL * chip_hops
    at_carried = jnp.where(on_line, line_pb, line_pa)
    at_other = jnp.where(diag, at_pa, jnp.where(on_line, line_pa, line_pb) + HOP_CORE)
    ready = jnp.maximum(jnp.maximum(at_carried, at_other), at_pb)
    steps = 2 * CHUNKS + ready

    def step(h, carry):
        def due(first):
            j = lax.div(h - first + 2, 2) - 1
            return j, (h >= first) & (j < CHUNKS) & (lax.rem(h - first + 2 * CHUNKS, 2) == 0)

        j_pa, do_pa = due(at_pa)

        @pl.when(do_pa & (r >= 2))
        def _():
            panel_got(pa, j_pa)
            send_panel(j_pa)

        @pl.when(do_pa & diag)
        def _():
            divide(pa, j_pa)
            left_copy(pa, j_pa, sibling, core_send).start()

        j_pb, do_pb = due(at_pb)

        @pl.when(do_pb & diag)
        def _():
            panel_got(pb, j_pb)
            divide(pb, j_pb)
            along(j_pb)
            left_copy(pb, j_pb, sibling, core_send).start()

        j_c, do_c = due(at_carried)

        @pl.when(do_c & jnp.logical_not(diag))
        def _():
            left_copy(pc, j_c, sibling, core_send).wait_recv()
            along(j_c)

            @pl.when(jnp.logical_not(at_source))
            def _():
                left_copy(pc, j_c, sibling, core_send).start()

        j_m, do_m = due(ready)

        @pl.when(do_m & jnp.logical_not(diag))
        def _():
            panel_got(pb, j_m)
            left_copy(po, j_m, sibling, core_send).wait_recv()

        @pl.when(do_m & (lax.rem(j_m, MERGE) == MERGE - 1))
        def _():
          first = pl.multiple_of((j_m - (MERGE - 1)) * chunk, MERGE * chunk)
          at = pl.ds(first, MERGE * chunk)
          factor = jnp.concatenate([left[p, at] for p in range(2)], axis=0)
          right = jnp.concatenate([panel[p, at] for p in range(2)], axis=0)
          out[...] = out[...] - contract0(factor, right)
        return carry

    lax.fori_loop(0, steps, step, 0)

    pltpu.make_async_copy(send.at[pl.ds(0, rows - 1)], recv.at[pl.ds(0, rows - 1)], t_send).wait()

    def drained(ref, sem):
        pltpu.make_async_copy(ref, ref, sem).wait()

    drained(panel.at[0], ax_send)

    @pl.when(r + 2 < rows)
    def _():
        drained(panel.at[0], ay_send)

    @pl.when(has_up)
    def _():
        drained(left.at[0], up_send)

    @pl.when(has_dn)
    def _():
        drained(left.at[0], dn_send)

    @pl.when(diag)
    def _():
        drained(left, core_send)

    @pl.when(jnp.logical_not(at_source))
    def _():
        drained(left.at[0], core_send)


def body(rows, cols, inverses, coupling, orders, owners, offsets, dense_slab, pivots):
    subs, order = inverses.shape[1], inverses.shape[2]
    width, tile = coupling.shape[3], dense_slab.shape[0]
    unit = (tile - width) // 2
    nb = width // unit
    packed = nb * nb // 2 * unit + nb // 2 * PAD
    panel_width = pivots.shape[0]
    assert nb % 2 == 0 and panel_width == 2 * tile and rows % 2 == 0 and cols % 2 == 0
    dma = pltpu.SemaphoreType.DMA
    hbm = pl.BlockSpec(memory_space=pl.ANY)
    smem = pl.BlockSpec(memory_space=pltpu.SMEM)
    vmem = pl.BlockSpec(memory_space=pltpu.VMEM)
    return pl.pallas_call(
        functools.partial(kernel, (rows, cols, subs, order, width, tile)),
        out_shape=pltpu.VMEM((tile, tile), F32),
        in_specs=[hbm, hbm, smem, smem, smem, hbm, vmem],
        out_specs=vmem,
        scratch_shapes=[
            pltpu.VMEM((subs, order, order), BF16),
            pltpu.VMEM((subs, order, width), BF16),
            pltpu.VMEM((tile, tile), F32),
            pltpu.VMEM((rows, packed, unit), BF16),
            pltpu.VMEM((rows, packed, unit), BF16),
            pltpu.VMEM((rows, (nb + 1) * (nb + 1), unit, unit), BF16),
            pltpu.VMEM((2, tile, tile), BF16),
            pltpu.VMEM((2, tile, tile), BF16),
            pltpu.VMEM((panel_width, 128), F32),
            dma((subs,)), dma((subs,)), dma(()),
            dma(()), dma((rows,)),
            dma(()), dma(()), dma((2, CHUNKS)),
            dma(()), dma(()), dma(()), dma((2, CHUNKS)),
        ],
        compiler_params=pltpu.CompilerParams(collective_id=0, has_side_effects=True),
    )(inverses, coupling, orders, jnp.transpose(owners, (0, 2, 1)),
      jnp.transpose(offsets, (0, 2, 1)), dense_slab, pivots.reshape(-1, 128))


def solution(mesh):
    placed = (
        P("row", "col", None, None),
        P("row", "col", None, None),
        P("row", "col"),
        P(None, "col", None),
        P(None, "col", None),
        P("row", "col"),
        P(),
    )
    return jax.shard_map(
        functools.partial(body, mesh.shape["row"], mesh.shape["col"]),
        mesh=mesh, in_specs=placed, out_specs=P("row", "col"), check_vma=False)
```

```python
import functools
import jax
import jax.numpy as jnp
from jax import lax
from jax.experimental import pallas as pl
from jax.experimental.pallas import tpu as pltpu
from jax.sharding import PartitionSpec as P

MESH = pl.DeviceIdType.MESH
BF16 = jnp.bfloat16
F32 = jnp.float32
CHUNKS = 16
MERGE = 2
AB = 256
PAD = 16
HOP_ROW = 4
HOP_COL = 4
HOP_CORE = 2


def contract0(a, b):
    return lax.dot_general(a, b, (((0,), (0,)), ((), ())), preferred_element_type=F32)


def kernel(
    dims,
    inv_hbm, cpl_hbm, orders_hbm, owners_hbm, offsets_hbm, slab_hbm, pivots_hbm,
    out,
    orders, owners, offsets, pivots,
    a_buf, m_buf, slab, send, recv, placed, panel, left, piv,
    a_sem, m_sem, s_sem, i_sem, t_send, t_recv, ax_send, ay_send, g_recv,
    up_send, dn_send, core_send, l_recv,
):
    rows, cols, subs, order, width, tile = dims
    unit = (tile - width) // 2
    nb = width // unit
    grid = tile // unit
    pairs = [(a, b) for a in range(nb) for b in range(a + 1, nb)]
    chunk = tile // CHUNKS
    ablocks = order // AB

    r = lax.axis_index("row")
    c = lax.axis_index("col")
    q, core = lax.div(c, 2), lax.rem(c, 2)
    chips = cols // 2
    q0, k0 = lax.div(r, 2), lax.rem(r, 2)
    pa = lax.rem(r, 2)
    pb = 1 - pa
    mate = r + 1 - 2 * pa
    sibling = c + 1 - 2 * core
    on_line = core == k0
    at_source = q == q0
    diag = at_source & on_line
    has_up = (q >= q0) & (q + 1 < chips)
    has_dn = (q <= q0) & (q > 0)
    chip_hops = jnp.where(q >= q0, q - q0, q0 - q)
    pc = jnp.where(on_line, pb, pa)
    po = 1 - pc

    def load_a(i):
        rows_i, cols_i = pl.ds(i * AB, AB), pl.ds(i * AB, order - i * AB)
        return pltpu.make_async_copy(
            inv_hbm.at[0, :, rows_i, cols_i], a_buf.at[:, rows_i, cols_i], a_sem)

    def wait_a():
        total = sum(AB * (order - i * AB) for i in range(ablocks)) // order
        pltpu.make_async_copy(
            inv_hbm.at[0, :, pl.ds(0, total)], a_buf.at[:, pl.ds(0, total)], a_sem).wait()

    load_m = pltpu.make_async_copy(cpl_hbm.at[0], m_buf, m_sem)
    load_slab = pltpu.make_async_copy(slab_hbm, slab, s_sem)
    small = [pltpu.make_async_copy(src, dst, i_sem.at[k]) for k, (src, dst) in enumerate(
        ((orders_hbm, orders), (owners_hbm, owners), (offsets_hbm, offsets), (pivots_hbm, pivots)))]
    load_m.start()
    for i in range(ablocks):
        load_a(i).start()
    for copy in small:
        copy.start()

    barrier = pltpu.get_barrier_semaphore()
    for t in range(rows):
        @pl.when(t != r)
        def _():
            pl.semaphore_signal(barrier, inc=1, device_id=(t, c), device_id_type=MESH)
    pl.semaphore_signal(barrier, inc=1, device_id=(r, sibling), device_id_type=MESH)

    @pl.when(q + 1 < chips)
    def _():
        pl.semaphore_signal(barrier, inc=1, device_id=(r, c + 2), device_id_type=MESH)

    @pl.when(q > 0)
    def _():
        pl.semaphore_signal(barrier, inc=1, device_id=(r, c - 2), device_id_type=MESH)

    def pick(src, dst):
        found, which = jnp.int32(0), jnp.int32(0)
        for s in range(subs):
            hit = owners[src, 0, s] == dst
            found, which = jnp.where(hit, 1, found), jnp.where(hit, s, which)
        return found, which

    def tile_copy(t, src_row):
        return pltpu.make_async_remote_copy(
            src_ref=send.at[t], dst_ref=recv.at[src_row],
            send_sem=t_send, recv_sem=t_recv.at[src_row],
            device_id=(t, c), device_id_type=MESH)

    above = (lax.broadcasted_iota(jnp.int32, (unit, unit), 0)
             <= lax.broadcasted_iota(jnp.int32, (unit, unit), 1))
    equal = (lax.broadcasted_iota(jnp.int32, (unit, unit), 0)
             == lax.broadcasted_iota(jnp.int32, (unit, unit), 1))

    def make_tile(which):
        live = lax.broadcasted_iota(jnp.int32, (order, width), 0) < orders[0, which]
        masked = jnp.where(live, m_buf[which], jnp.zeros((order, width), BF16))
        pieces = []
        for i in range(ablocks):
            lo, hi = i * AB, (i + 1) * AB
            half = a_buf[which, lo:hi, lo:hi] * jnp.asarray(0.5, BF16)
            piece = jnp.dot(half, masked[lo:hi], preferred_element_type=F32)
            if hi < order:
                piece = piece + jnp.dot(a_buf[which, lo:hi, hi:], masked[hi:],
                                        preferred_element_type=F32)
            pieces.append(piece.astype(BF16))
        half_tile = contract0(masked, jnp.concatenate(pieces, axis=0))

        def block(a, b):
            return half_tile[a * unit:(a + 1) * unit, b * unit:(b + 1) * unit]

        def whole(a, b):
            return block(a, b) + jnp.transpose(block(b, a))

        stored = [jnp.where(above, whole(a, a), whole(a + 1, a + 1)) for a in range(0, nb, 2)]
        stored += [whole(a, b) for a, b in pairs]
        stored += [jnp.broadcast_to(jnp.sum(jnp.where(equal, 2 * block(a, a), 0.0), axis=0, keepdims=True),
                                    (PAD, unit)) for a in range(1, nb, 2)]
        return jnp.concatenate(stored, axis=0).astype(BF16)

    load_m.wait()
    wait_a()
    for copy in small:
        copy.wait()
    load_slab.start()

    neighbours = rows + jnp.where(q + 1 < chips, 1, 0) + jnp.where(q > 0, 1, 0)
    pl.semaphore_wait(barrier, neighbours)

    others = rows - 2
    for u in range(rows):
        if u == 0:
            t = pb
        elif u == rows - 1:
            t = r
        else:
            far = jnp.where(r < 2, 2 + lax.rem(u - 1 + pa, others), 2 + lax.rem(r - 2 + u - 1, others))
            t = jnp.where(r >= 2, pa, far) if u == 1 else far
        _, which = pick(r, t)
        value = make_tile(which)
        if u < rows - 1:
            send[t] = value
            tile_copy(t, r).start()
        else:
            recv[t] = value

    for k in range(pivots.shape[0]):
        piv[pl.ds(k * 128, 128), :] = jnp.transpose(
            jnp.broadcast_to(pivots[pl.ds(k, 1), :], (128, 128)))
    for t in range(rows):
        for k in range(nb + 1):
            placed[t, k * (nb + 1) + nb] = jnp.zeros((unit, unit), BF16)
            placed[t, nb * (nb + 1) + k] = jnp.zeros((unit, unit), BF16)


    def part(ref, p, j):
        return ref.at[p, pl.ds(pl.multiple_of(j * chunk, chunk), chunk)]

    def panel_copy(j, target, sem):
        return pltpu.make_async_remote_copy(
            src_ref=part(panel, pa, j), dst_ref=part(panel, pa, j),
            send_sem=sem, recv_sem=g_recv.at[pa, j],
            device_id=(target, c), device_id_type=MESH)

    def panel_got(p, j):
        pltpu.make_async_remote_copy(
            src_ref=part(panel, p, j), dst_ref=part(panel, p, j),
            send_sem=ax_send, recv_sem=g_recv.at[p, j],
            device_id=(mate, c), device_id_type=MESH).wait_recv()

    def send_panel(j):
        @pl.when(r + 2 < rows)
        def _():
            panel_copy(j, r + 2, ay_send).start()
        panel_copy(j, mate, ax_send).start()

    def left_copy(p, j, target, sem):
        return pltpu.make_async_remote_copy(
            src_ref=part(left, p, j), dst_ref=part(left, p, j),
            send_sem=sem, recv_sem=l_recv.at[p, j],
            device_id=(r, target), device_id_type=MESH)

    def along(j):
        @pl.when(has_up)
        def _():
            left_copy(pc, j, c + 2, up_send).start()

        @pl.when(has_dn)
        def _():
            left_copy(pc, j, c - 2, dn_send).start()

    lanes = tile // 128

    def divide(p, j):
        at = pl.ds(pl.multiple_of(j * chunk, chunk), chunk)
        pivot = piv[pl.ds(pl.multiple_of(p * tile + j * chunk, chunk), chunk), :]
        raw = panel[p, at].astype(F32)
        left[p, at] = (raw / jnp.concatenate([pivot] * lanes, axis=1)).astype(BF16)

    load_slab.wait()
    places = []
    side = nb + 1
    for t in range(rows):
        found, which = pick(t, r)
        at_row, at_col = offsets[t, 0, which], offsets[t, 1, which]
        spots = []
        for start in (at_row, at_col):
            inside = [(found > 0) & (k - start >= 0) & (k - start < nb) for k in range(grid)]
            spots.append([jnp.where(ok, k - start, nb) for k, ok in enumerate(inside)])
        places.append(([side * a for a in spots[0]], spots[1]))

        @pl.when(t != r)
        def _():
            tile_copy(t, t).wait_recv()
    for t in range(rows):
        for k in range(nb // 2):
            pack = recv[t, k * unit:(k + 1) * unit].astype(F32)
            flip = jnp.transpose(pack)
            at = (nb // 2 + len(pairs)) * unit + k * PAD
            line = jnp.concatenate([recv[t, at:at + PAD]] * (unit // PAD), axis=0).astype(F32)
            a = 2 * k
            placed[t, a * side + a] = jnp.where(above, pack, flip).astype(BF16)
            low = jnp.where(above, flip, pack)
            placed[t, (a + 1) * side + a + 1] = jnp.where(equal, line, low).astype(BF16)
        for k, (a, b) in enumerate(pairs):
            at = (nb // 2 + k) * unit
            value = recv[t, at:at + unit]
            placed[t, a * side + b] = value
            placed[t, b * side + a] = jnp.transpose(value.astype(F32)).astype(BF16)
    for i in range(grid):
        for j in range(grid):
            total = slab[i * unit:(i + 1) * unit, j * unit:(j + 1) * unit]
            for t in range(rows):
                total = total - placed[t, places[t][0][i] + places[t][1][j]].astype(F32)
            out[i * unit:(i + 1) * unit, j * unit:(j + 1) * unit] = total

        @pl.when(r < 2)
        def _():
            span = slice(i * unit, (i + 1) * unit)
            panel[pa, span] = out[span, :].astype(BF16)
            for j in range(i * unit // chunk, (i + 1) * unit // chunk):
                send_panel(j)

    row_hops = lax.div(r, 2)
    at_pa = HOP_ROW * row_hops
    at_pb = at_pa + HOP_ROW
    line_pa = at_pa + HOP_CORE + HOP_COL * chip_hops
    line_pb = at_pb + HOP_COL * chip_hops
    at_carried = jnp.where(on_line, line_pb, line_pa)
    at_other = jnp.where(diag, at_pa, jnp.where(on_line, line_pa, line_pb) + HOP_CORE)
    ready = jnp.maximum(jnp.maximum(at_carried, at_other), at_pb)
    steps = CHUNKS + ready

    def step(h, carry):
        def due(first):
            j = h - first
            return j, (j >= 0) & (j < CHUNKS)

        j_pa, do_pa = due(at_pa)

        @pl.when(do_pa & (r >= 2))
        def _():
            panel_got(pa, j_pa)
            send_panel(j_pa)

        @pl.when(do_pa & diag)
        def _():
            divide(pa, j_pa)
            left_copy(pa, j_pa, sibling, core_send).start()

        j_pb, do_pb = due(at_pb)

        @pl.when(do_pb & diag)
        def _():
            panel_got(pb, j_pb)
            divide(pb, j_pb)
            along(j_pb)
            left_copy(pb, j_pb, sibling, core_send).start()

        j_c, do_c = due(at_carried)

        @pl.when(do_c & jnp.logical_not(diag))
        def _():
            left_copy(pc, j_c, sibling, core_send).wait_recv()
            along(j_c)

            @pl.when(jnp.logical_not(at_source))
            def _():
                left_copy(pc, j_c, sibling, core_send).start()

        j_m, do_m = due(ready)

        @pl.when(do_m & jnp.logical_not(diag))
        def _():
            panel_got(pb, j_m)
            left_copy(po, j_m, sibling, core_send).wait_recv()

        @pl.when(do_m & (lax.rem(j_m, MERGE) == MERGE - 1))
        def _():
          first = pl.multiple_of((j_m - (MERGE - 1)) * chunk, MERGE * chunk)
          at = pl.ds(first, MERGE * chunk)
          factor = jnp.concatenate([left[p, at] for p in range(2)], axis=0)
          right = jnp.concatenate([panel[p, at] for p in range(2)], axis=0)
          out[...] = out[...] - contract0(factor, right)
        return carry

    lax.fori_loop(0, steps, step, 0)

    pltpu.make_async_copy(send.at[pl.ds(0, rows - 1)], recv.at[pl.ds(0, rows - 1)], t_send).wait()

    def drained(ref, sem):
        pltpu.make_async_copy(ref, ref, sem).wait()

    drained(panel.at[0], ax_send)

    @pl.when(r + 2 < rows)
    def _():
        drained(panel.at[0], ay_send)

    @pl.when(has_up)
    def _():
        drained(left.at[0], up_send)

    @pl.when(has_dn)
    def _():
        drained(left.at[0], dn_send)

    @pl.when(diag)
    def _():
        drained(left, core_send)

    @pl.when(jnp.logical_not(at_source))
    def _():
        drained(left.at[0], core_send)


def body(rows, cols, inverses, coupling, orders, owners, offsets, dense_slab, pivots):
    subs, order = inverses.shape[1], inverses.shape[2]
    width, tile = coupling.shape[3], dense_slab.shape[0]
    unit = (tile - width) // 2
    nb = width // unit
    packed = nb * nb // 2 * unit + nb // 2 * PAD
    panel_width = pivots.shape[0]
    assert nb % 2 == 0 and panel_width == 2 * tile and rows % 2 == 0 and cols % 2 == 0
    dma = pltpu.SemaphoreType.DMA
    hbm = pl.BlockSpec(memory_space=pl.ANY)
    vmem = pl.BlockSpec(memory_space=pltpu.VMEM)
    return pl.pallas_call(
        functools.partial(kernel, (rows, cols, subs, order, width, tile)),
        out_shape=pltpu.VMEM((tile, tile), F32),
        in_specs=[hbm] * 7,
        out_specs=vmem,
        scratch_shapes=[
            pltpu.SMEM(orders.shape, jnp.int32),
            pltpu.SMEM((owners.shape[0], owners.shape[2], owners.shape[1]), jnp.int32),
            pltpu.SMEM((offsets.shape[0], offsets.shape[2], offsets.shape[1]), jnp.int32),
            pltpu.VMEM((panel_width // 128, 128), F32),
            pltpu.VMEM((subs, order, order), BF16),
            pltpu.VMEM((subs, order, width), BF16),
            pltpu.VMEM((tile, tile), F32),
            pltpu.VMEM((rows, packed, unit), BF16),
            pltpu.VMEM((rows, packed, unit), BF16),
            pltpu.VMEM((rows, (nb + 1) * (nb + 1), unit, unit), BF16),
            pltpu.VMEM((2, tile, tile), BF16),
            pltpu.VMEM((2, tile, tile), BF16),
            pltpu.VMEM((panel_width, 128), F32),
            dma(()), dma(()), dma(()), dma((4,)),
            dma(()), dma((rows,)),
            dma(()), dma(()), dma((2, CHUNKS)),
            dma(()), dma(()), dma(()), dma((2, CHUNKS)),
        ],
        compiler_params=pltpu.CompilerParams(collective_id=0, has_side_effects=True),
    )(inverses, coupling, orders, jnp.transpose(owners, (0, 2, 1)),
      jnp.transpose(offsets, (0, 2, 1)), dense_slab, pivots.reshape(-1, 128))


def solution(mesh):
    placed = (
        P("row", "col", None, None),
        P("row", "col", None, None),
        P("row", "col"),
        P(None, "col", None),
        P(None, "col", None),
        P("row", "col"),
        P(),
    )
    return jax.shard_map(
        functools.partial(body, mesh.shape["row"], mesh.shape["col"]),
        mesh=mesh, in_specs=placed, out_specs=P("row", "col"), check_vma=False)
```

```python
import functools
import jax
import jax.numpy as jnp
from jax import lax
from jax.experimental import pallas as pl
from jax.experimental.pallas import tpu as pltpu
from jax.sharding import PartitionSpec as P

MESH = pl.DeviceIdType.MESH
BF16 = jnp.bfloat16
F32 = jnp.float32
CHUNKS = 16
MERGE = 2
AB = 256
PAD = 16
HOP_ROW = 2
HOP_MATE = 4
HOP_COL = 4
HOP_CORE = 3


def contract0(a, b):
    return lax.dot_general(a, b, (((0,), (0,)), ((), ())), preferred_element_type=F32)


def kernel(
    dims,
    inv_hbm, cpl_hbm, orders_hbm, owners_hbm, offsets_hbm, slab_hbm, pivots_hbm,
    out,
    orders, owners, offsets, pivots,
    a_buf, m_buf, slab, send, recv, placed, panel, left, piv,
    a_sem, m_sem, s_sem, i_sem, t_send, t_recv, ax_send, ay_send, g_recv,
    up_send, dn_send, core_send, l_recv,
):
    rows, cols, subs, order, width, tile = dims
    unit = (tile - width) // 2
    nb = width // unit
    grid = tile // unit
    pairs = [(a, b) for a in range(nb) for b in range(a + 1, nb)]
    chunk = tile // CHUNKS
    ablocks = order // AB

    r = lax.axis_index("row")
    c = lax.axis_index("col")
    q, core = lax.div(c, 2), lax.rem(c, 2)
    chips = cols // 2
    q0, k0 = lax.div(r, 2), lax.rem(r, 2)
    pa = lax.rem(r, 2)
    pb = 1 - pa
    mate = r + 1 - 2 * pa
    sibling = c + 1 - 2 * core
    on_line = core == k0
    at_source = q == q0
    diag = at_source & on_line
    has_up = (q >= q0) & (q + 1 < chips)
    has_dn = (q <= q0) & (q > 0)
    chip_hops = jnp.where(q >= q0, q - q0, q0 - q)
    pc = jnp.where(on_line, pb, pa)
    po = 1 - pc

    def load_a(i):
        rows_i, cols_i = pl.ds(i * AB, AB), pl.ds(i * AB, order - i * AB)
        return pltpu.make_async_copy(
            inv_hbm.at[0, :, rows_i, cols_i], a_buf.at[:, rows_i, cols_i], a_sem)

    def wait_a():
        total = sum(AB * (order - i * AB) for i in range(ablocks)) // order
        pltpu.make_async_copy(
            inv_hbm.at[0, :, pl.ds(0, total)], a_buf.at[:, pl.ds(0, total)], a_sem).wait()

    load_m = pltpu.make_async_copy(cpl_hbm.at[0], m_buf, m_sem)
    load_slab = pltpu.make_async_copy(slab_hbm, slab, s_sem)
    small = [pltpu.make_async_copy(src, dst, i_sem.at[k]) for k, (src, dst) in enumerate(
        ((orders_hbm, orders), (owners_hbm, owners), (offsets_hbm, offsets), (pivots_hbm, pivots)))]
    load_m.start()
    for i in range(ablocks):
        load_a(i).start()
    for copy in small:
        copy.start()

    barrier = pltpu.get_barrier_semaphore()
    for t in range(rows):
        @pl.when(t != r)
        def _():
            pl.semaphore_signal(barrier, inc=1, device_id=(t, c), device_id_type=MESH)
    pl.semaphore_signal(barrier, inc=1, device_id=(r, sibling), device_id_type=MESH)

    @pl.when(q + 1 < chips)
    def _():
        pl.semaphore_signal(barrier, inc=1, device_id=(r, c + 2), device_id_type=MESH)

    @pl.when(q > 0)
    def _():
        pl.semaphore_signal(barrier, inc=1, device_id=(r, c - 2), device_id_type=MESH)

    def pick(src, dst):
        found, which = jnp.int32(0), jnp.int32(0)
        for s in range(subs):
            hit = owners[src, 0, s] == dst
            found, which = jnp.where(hit, 1, found), jnp.where(hit, s, which)
        return found, which

    def tile_copy(t, src_row):
        return pltpu.make_async_remote_copy(
            src_ref=send.at[t], dst_ref=recv.at[src_row],
            send_sem=t_send, recv_sem=t_recv.at[src_row],
            device_id=(t, c), device_id_type=MESH)

    above = (lax.broadcasted_iota(jnp.int32, (unit, unit), 0)
             <= lax.broadcasted_iota(jnp.int32, (unit, unit), 1))
    equal = (lax.broadcasted_iota(jnp.int32, (unit, unit), 0)
             == lax.broadcasted_iota(jnp.int32, (unit, unit), 1))

    def make_tile(which):
        live = lax.broadcasted_iota(jnp.int32, (order, width), 0) < orders[0, which]
        masked = jnp.where(live, m_buf[which], jnp.zeros((order, width), BF16))
        pieces = []
        for i in range(ablocks):
            lo, hi = i * AB, (i + 1) * AB
            half = a_buf[which, lo:hi, lo:hi] * jnp.asarray(0.5, BF16)
            piece = jnp.dot(half, masked[lo:hi], preferred_element_type=F32)
            if hi < order:
                piece = piece + jnp.dot(a_buf[which, lo:hi, hi:], masked[hi:],
                                        preferred_element_type=F32)
            pieces.append(piece.astype(BF16))
        half_tile = contract0(masked, jnp.concatenate(pieces, axis=0))

        def block(a, b):
            return half_tile[a * unit:(a + 1) * unit, b * unit:(b + 1) * unit]

        def whole(a, b):
            return block(a, b) + jnp.transpose(block(b, a))

        stored = [jnp.where(above, whole(a, a), whole(a + 1, a + 1)) for a in range(0, nb, 2)]
        stored += [whole(a, b) for a, b in pairs]
        stored += [jnp.broadcast_to(jnp.sum(jnp.where(equal, 2 * block(a, a), 0.0), axis=0, keepdims=True),
                                    (PAD, unit)) for a in range(1, nb, 2)]
        return jnp.concatenate(stored, axis=0).astype(BF16)

    load_m.wait()
    wait_a()
    for copy in small:
        copy.wait()
    load_slab.start()

    neighbours = rows + jnp.where(q + 1 < chips, 1, 0) + jnp.where(q > 0, 1, 0)
    pl.semaphore_wait(barrier, neighbours)

    others = rows - 2
    for u in range(rows):
        if u == 0:
            t = pb
        elif u == rows - 1:
            t = r
        else:
            far = jnp.where(r < 2, 2 + lax.rem(u - 1 + pa, others), 2 + lax.rem(r - 2 + u - 1, others))
            t = jnp.where(r >= 2, pa, far) if u == 1 else far
        _, which = pick(r, t)
        value = make_tile(which)
        if u < rows - 1:
            send[t] = value
            tile_copy(t, r).start()
        else:
            recv[t] = value

    for k in range(pivots.shape[0]):
        piv[pl.ds(k * 128, 128), :] = jnp.transpose(
            jnp.broadcast_to(pivots[pl.ds(k, 1), :], (128, 128)))
    for t in range(rows):
        for k in range(nb + 1):
            placed[t, k * (nb + 1) + nb] = jnp.zeros((unit, unit), BF16)
            placed[t, nb * (nb + 1) + k] = jnp.zeros((unit, unit), BF16)


    def part(ref, p, j):
        return ref.at[p, pl.ds(pl.multiple_of(j * chunk, chunk), chunk)]

    def panel_copy(j, target, sem):
        return pltpu.make_async_remote_copy(
            src_ref=part(panel, pa, j), dst_ref=part(panel, pa, j),
            send_sem=sem, recv_sem=g_recv.at[pa, j],
            device_id=(target, c), device_id_type=MESH)

    def panel_got(p, j):
        pltpu.make_async_remote_copy(
            src_ref=part(panel, p, j), dst_ref=part(panel, p, j),
            send_sem=ax_send, recv_sem=g_recv.at[p, j],
            device_id=(mate, c), device_id_type=MESH).wait_recv()

    def send_panel(j):
        @pl.when(r + 2 < rows)
        def _():
            panel_copy(j, r + 2, ay_send).start()
        panel_copy(j, mate, ax_send).start()

    def left_copy(p, j, target, sem):
        return pltpu.make_async_remote_copy(
            src_ref=part(left, p, j), dst_ref=part(left, p, j),
            send_sem=sem, recv_sem=l_recv.at[p, j],
            device_id=(r, target), device_id_type=MESH)

    def along(j):
        @pl.when(has_up)
        def _():
            left_copy(pc, j, c + 2, up_send).start()

        @pl.when(has_dn)
        def _():
            left_copy(pc, j, c - 2, dn_send).start()

    lanes = tile // 128

    def divide(p, j):
        at = pl.ds(pl.multiple_of(j * chunk, chunk), chunk)
        pivot = piv[pl.ds(pl.multiple_of(p * tile + j * chunk, chunk), chunk), :]
        raw = panel[p, at].astype(F32)
        left[p, at] = (raw / jnp.concatenate([pivot] * lanes, axis=1)).astype(BF16)

    load_slab.wait()
    places = []
    side = nb + 1
    for t in range(rows):
        found, which = pick(t, r)
        at_row, at_col = offsets[t, 0, which], offsets[t, 1, which]
        spots = []
        for start in (at_row, at_col):
            inside = [(found > 0) & (k - start >= 0) & (k - start < nb) for k in range(grid)]
            spots.append([jnp.where(ok, k - start, nb) for k, ok in enumerate(inside)])
        places.append(([side * a for a in spots[0]], spots[1]))

        @pl.when(t != r)
        def _():
            tile_copy(t, t).wait_recv()
    for t in range(rows):
        for k in range(nb // 2):
            pack = recv[t, k * unit:(k + 1) * unit].astype(F32)
            flip = jnp.transpose(pack)
            at = (nb // 2 + len(pairs)) * unit + k * PAD
            line = jnp.concatenate([recv[t, at:at + PAD]] * (unit // PAD), axis=0).astype(F32)
            a = 2 * k
            placed[t, a * side + a] = jnp.where(above, pack, flip).astype(BF16)
            low = jnp.where(above, flip, pack)
            placed[t, (a + 1) * side + a + 1] = jnp.where(equal, line, low).astype(BF16)
        for k, (a, b) in enumerate(pairs):
            at = (nb // 2 + k) * unit
            value = recv[t, at:at + unit]
            placed[t, a * side + b] = value
            placed[t, b * side + a] = jnp.transpose(value.astype(F32)).astype(BF16)
    for i in range(grid):
        for j in range(grid):
            total = slab[i * unit:(i + 1) * unit, j * unit:(j + 1) * unit]
            for t in range(rows):
                total = total - placed[t, places[t][0][i] + places[t][1][j]].astype(F32)
            out[i * unit:(i + 1) * unit, j * unit:(j + 1) * unit] = total

        @pl.when(r < 2)
        def _():
            span = slice(i * unit, (i + 1) * unit)
            panel[pa, span] = out[span, :].astype(BF16)
            for j in range(i * unit // chunk, (i + 1) * unit // chunk):
                send_panel(j)

    row_hops = lax.div(r, 2)
    at_pa = HOP_ROW * row_hops
    at_pb = at_pa + HOP_MATE
    line_pa = at_pa + HOP_CORE + HOP_COL * chip_hops
    line_pb = at_pb + HOP_COL * chip_hops
    at_carried = jnp.where(on_line, line_pb, line_pa)
    at_other = jnp.where(diag, at_pa, jnp.where(on_line, line_pa, line_pb) + HOP_CORE)
    ready = jnp.maximum(jnp.maximum(at_carried, at_other), at_pb)
    steps = CHUNKS + ready

    def step(h, carry):
        def due(first):
            j = h - first
            return j, (j >= 0) & (j < CHUNKS)

        j_pa, do_pa = due(at_pa)

        @pl.when(do_pa & (r >= 2))
        def _():
            panel_got(pa, j_pa)
            send_panel(j_pa)

        @pl.when(do_pa & diag)
        def _():
            divide(pa, j_pa)
            left_copy(pa, j_pa, sibling, core_send).start()

        j_pb, do_pb = due(at_pb)

        @pl.when(do_pb & diag)
        def _():
            panel_got(pb, j_pb)
            divide(pb, j_pb)
            along(j_pb)
            left_copy(pb, j_pb, sibling, core_send).start()

        j_c, do_c = due(at_carried)

        @pl.when(do_c & jnp.logical_not(diag))
        def _():
            left_copy(pc, j_c, sibling, core_send).wait_recv()
            along(j_c)

            @pl.when(jnp.logical_not(at_source))
            def _():
                left_copy(pc, j_c, sibling, core_send).start()

        j_m, do_m = due(ready)

        @pl.when(do_m & jnp.logical_not(diag))
        def _():
            panel_got(pb, j_m)
            left_copy(po, j_m, sibling, core_send).wait_recv()

        @pl.when(do_m & (lax.rem(j_m, MERGE) == MERGE - 1))
        def _():
          first = pl.multiple_of((j_m - (MERGE - 1)) * chunk, MERGE * chunk)
          at = pl.ds(first, MERGE * chunk)
          factor = jnp.concatenate([left[p, at] for p in range(2)], axis=0)
          right = jnp.concatenate([panel[p, at] for p in range(2)], axis=0)
          out[...] = out[...] - contract0(factor, right)
        return carry

    lax.fori_loop(0, steps, step, 0)

    pltpu.make_async_copy(send.at[pl.ds(0, rows - 1)], recv.at[pl.ds(0, rows - 1)], t_send).wait()

    def drained(ref, sem):
        pltpu.make_async_copy(ref, ref, sem).wait()

    drained(panel.at[0], ax_send)

    @pl.when(r + 2 < rows)
    def _():
        drained(panel.at[0], ay_send)

    @pl.when(has_up)
    def _():
        drained(left.at[0], up_send)

    @pl.when(has_dn)
    def _():
        drained(left.at[0], dn_send)

    @pl.when(diag)
    def _():
        drained(left, core_send)

    @pl.when(jnp.logical_not(at_source))
    def _():
        drained(left.at[0], core_send)


def body(rows, cols, inverses, coupling, orders, owners, offsets, dense_slab, pivots):
    subs, order = inverses.shape[1], inverses.shape[2]
    width, tile = coupling.shape[3], dense_slab.shape[0]
    unit = (tile - width) // 2
    nb = width // unit
    packed = nb * nb // 2 * unit + nb // 2 * PAD
    panel_width = pivots.shape[0]
    assert nb % 2 == 0 and panel_width == 2 * tile and rows % 2 == 0 and cols % 2 == 0
    dma = pltpu.SemaphoreType.DMA
    hbm = pl.BlockSpec(memory_space=pl.ANY)
    vmem = pl.BlockSpec(memory_space=pltpu.VMEM)
    return pl.pallas_call(
        functools.partial(kernel, (rows, cols, subs, order, width, tile)),
        out_shape=pltpu.VMEM((tile, tile), F32),
        in_specs=[hbm] * 7,
        out_specs=vmem,
        scratch_shapes=[
            pltpu.SMEM(orders.shape, jnp.int32),
            pltpu.SMEM((owners.shape[0], owners.shape[2], owners.shape[1]), jnp.int32),
            pltpu.SMEM((offsets.shape[0], offsets.shape[2], offsets.shape[1]), jnp.int32),
            pltpu.VMEM((panel_width // 128, 128), F32),
            pltpu.VMEM((subs, order, order), BF16),
            pltpu.VMEM((subs, order, width), BF16),
            pltpu.VMEM((tile, tile), F32),
            pltpu.VMEM((rows, packed, unit), BF16),
            pltpu.VMEM((rows, packed, unit), BF16),
            pltpu.VMEM((rows, (nb + 1) * (nb + 1), unit, unit), BF16),
            pltpu.VMEM((2, tile, tile), BF16),
            pltpu.VMEM((2, tile, tile), BF16),
            pltpu.VMEM((panel_width, 128), F32),
            dma(()), dma(()), dma(()), dma((4,)),
            dma(()), dma((rows,)),
            dma(()), dma(()), dma((2, CHUNKS)),
            dma(()), dma(()), dma(()), dma((2, CHUNKS)),
        ],
        compiler_params=pltpu.CompilerParams(collective_id=0, has_side_effects=True),
    )(inverses, coupling, orders, jnp.transpose(owners, (0, 2, 1)),
      jnp.transpose(offsets, (0, 2, 1)), dense_slab, pivots.reshape(-1, 128))


def solution(mesh):
    placed = (
        P("row", "col", None, None),
        P("row", "col", None, None),
        P("row", "col"),
        P(None, "col", None),
        P(None, "col", None),
        P("row", "col"),
        P(),
    )
    return jax.shard_map(
        functools.partial(body, mesh.shape["row"], mesh.shape["col"]),
        mesh=mesh, in_specs=placed, out_specs=P("row", "col"), check_vma=False)
```
